32 devices in a mesh: dp: 4 (over y, x), expert: 8 (over z, core).
Axes of the slice: x: 2, y: 2, z: 4, core: 2. Of those that a mesh axis runs over, the one named last changes fastest.
Arguments:
- tokens: bfloat16 [4096, 2048], P(('dp', 'expert')), may hold values from -6 to 6
- cotangent: bfloat16 [4096, 2048], P(('dp', 'expert')), may hold values from -6 to 6
- expert_ids: int32 [4096, 8], P(('dp', 'expert')), may hold values from 0 to 15, all different within a row; in each aligned block of 128 rows (0 to 127, 128 to 255, ...) at most 80 rows name the same one
- combine: float32 [4096, 8], P(('dp', 'expert')), may hold values from 0.05 to 0.3
- placement: int32 [16], replicated, may hold values from 0 to 15, each once
- swap_slots: int32 [8], replicated, may hold values from 0 to 1
- gate_weight: bfloat16 [16, 768, 2048], P('expert', None, 'dp'), may hold values from -0.125 to 0.125
- up_weight: bfloat16 [16, 768, 2048], P('expert', None, 'dp'), may hold values from -0.125 to 0.125
- moment_first: float32 [2048, 16, 768], P('dp', 'expert'), may hold values from -12 to 12
- moment_second: float32 [2048, 16, 768], P('dp', 'expert'), may hold values from 1 to 100
Outputs:
- gate_moved: bfloat16 [16, 768, 2048], P('expert', None, 'dp')
- up_moved: bfloat16 [16, 768, 2048], P('expert', None, 'dp')
- first_new: float32 [2048, 16, 768], P('dp', 'expert')
- second_new: float32 [2048, 16, 768], P('dp', 'expert')
- update: float32 [2048, 16, 768], P('dp', 'expert')
The draws below stay inside these ranges and needn't reach their ends.
Inputs may be any that keep to these rules, and one draw needn't show every extreme that they name: `expert_ids`: each token names 8 different experts; the rows of one device name no expert more than 80 times. `placement`: a permutation of the experts over the slots.
All inputs are finite; a program needn't handle non-finite values.
Results may differ from the reference program's by a relative error of at most 0.0075.
Values may be sent and summed in bfloat16 or wider, within the bound.
No kernel may reach another device: no remote copies, remote signals or barrier semaphores. Data moves between devices by JAX's collectives and lax.ppermute only.
A program may use at most 128 MiB of HBM per device.

```python
import math
import jax
import jax.numpy as jnp
import numpy as np
from jax import lax

D = 2048
H = 768
TOPK = 8
EXP_DEV = 2
TOK_DEV = 128
EXPERTS = 16
HOLDERS = 8
CAP = 80
TOKENS = 4096
N_DP = 4


def place_ends(drawn, key, low, top_value):
    longest = drawn.shape.index(max(drawn.shape))
    spots = []
    for shift in (0, 1):
        where = [jax.random.randint(jax.random.fold_in(key, axis), (), 0, length) for axis, length in enumerate(drawn.shape)]
        where[longest] = (where[longest] + shift) % drawn.shape[longest]
        spots.append(tuple(where))
    return drawn.at[spots[0]].set(low).at[spots[1]].set(top_value)


def shard_levels(stream_key, shape, split, least, top_value):
    level, own = 1.0, jax.random.fold_in(stream_key, 6)
    for axis_at, parts in split:
        draws = jnp.exp(jax.random.uniform(jax.random.fold_in(own, axis_at), (parts,), jnp.float32, least / len(split), top_value / len(split)))
        level = level * jnp.repeat(draws, shape[axis_at] // parts).reshape([-1 if axis == axis_at else 1 for axis in range(len(shape))])
    return level


def routed_block(stream_key, own, number, rows, amount, top, limit, slope):
    order = jax.random.permutation(stream_key, amount)
    heavy_load, common = portions_of(amount, rows * top, limit, slope, True), portions_of(amount, rows * top, limit, slope, False)
    places = jnp.arange(amount)

    def named(sizes, offset_by):
        used = int((sizes > 0).sum())
        fixed = max(1, used // 4)
        passed = fixed + (places - fixed + offset_by * (used - fixed)) % max(1, amount - fixed)
        return jnp.zeros((amount,), jnp.int32).at[order[jnp.where(places < fixed, places, passed)]].set(jnp.asarray(sizes, jnp.int32))

    sizes = jnp.where(number % 4 == 0, named(heavy_load, number // 4), named(common, number - number // 4 - 1))
    mixed = jax.random.permutation(jax.random.fold_in(own, 3), amount)
    donor, sink = mixed[0:amount // 2 * 2:2], mixed[1:amount // 2 * 2:2]
    room = jnp.minimum(sizes[donor] - 1, limit - sizes[sink]) // 2
    room = jnp.where((donor == order[0]) | (sink == order[0]) | (sizes[sink] == 0), 0, jnp.maximum(room, 0))
    passed = jax.random.randint(jax.random.fold_in(own, 4), (amount // 2,), 0, 1 << 20) % (room + 1)
    sizes = sizes.at[donor].add(-passed).at[sink].add(passed)
    labels = jnp.searchsorted(jnp.cumsum(sizes), jnp.arange(rows * top), side="right").astype(jnp.int32)
    grid = labels.reshape(top, rows).T
    grid = grid[jax.random.permutation(jax.random.fold_in(own, 1), rows)]
    offset_by = jax.random.randint(jax.random.fold_in(own, 2), (rows, 1), 0, top)
    return jnp.take_along_axis(grid, (jnp.arange(top)[None, :] + offset_by) % top, axis=1)


def portions_of(number_of, total, reach, lean, full):
    weights = [(1 << 20) // math.isqrt(standing ** lean) + 1 for standing in range(1, number_of + 1)]
    largest = reach if full else min(reach, max(-(-total // number_of), total * weights[0] // sum(weights)))
    least = 1 if total - largest >= number_of - 1 else 0
    given, rest = [largest] + [least] * (number_of - 1), total - largest - least * (number_of - 1)
    while rest > 0:
        free = [i for i in range(1, number_of) if given[i] < largest] or [i for i in range(1, number_of) if given[i] < reach]
        pool, remaining = sum([weights[i] for i in free]), rest
        for i in free:
            extra = min(reach - given[i], max(1, remaining * weights[i] // pool), rest)
            given[i] = given[i] + extra
            rest = rest - extra
    return np.array(given)


def centred(key, extent, spread, reach, cuts=(), held_as=jnp.bfloat16):
    values = spread * jax.random.normal(key, extent, jnp.float32)
    if cuts:
        values = values * shard_levels(key, extent, cuts, -0.22, 0.18)
    return jnp.clip(values, -reach, reach).astype(held_as)


def setup_inputs(seed: int = 0) -> dict:
    arg_keys = jax.random.split(jax.random.key(seed), 11)
    tokens = centred(arg_keys[0], (TOKENS, D), 1.0, 6.0, ((0, 32),))
    cotangent = centred(arg_keys[1], (TOKENS, D), 1.0, 6.0, ((0, 32),))
    expert_ids_keys = jax.random.split(jax.random.fold_in(arg_keys[2], 1), TOKENS // TOK_DEV)
    expert_ids_turns = jax.random.permutation(jax.random.fold_in(arg_keys[2], 3), TOKENS // TOK_DEV)
    expert_ids = jax.vmap(lambda own, number: routed_block(jax.random.fold_in(arg_keys[2], 2), own, number, TOK_DEV, EXPERTS, TOPK, CAP, 1))(expert_ids_keys, expert_ids_turns).reshape((TOKENS, TOPK))
    combine = jnp.clip(0.05 + 0.25 * jax.random.uniform(arg_keys[3], (TOKENS, TOPK), jnp.float32) ** shard_levels(arg_keys[3], (TOKENS, TOPK), ((0, 32),), -0.2, 0.2), 0.05, 0.3)
    placement = jax.random.permutation(arg_keys[4], EXPERTS).astype(jnp.int32)
    swap_slots = place_ends(jax.random.randint(arg_keys[5], (HOLDERS,), 0, EXP_DEV), jax.random.fold_in(arg_keys[5], 1), 0, EXP_DEV - 1).astype(jnp.int32)
    gate_weight = centred(arg_keys[6], (EXPERTS, H, D), D ** -0.5, 0.125, ((0, 8), (2, 4)))
    up_weight = centred(arg_keys[7], (EXPERTS, H, D), D ** -0.5, 0.125, ((0, 8), (2, 4)))
    moment_first = centred(arg_keys[8], (D, EXPERTS, H), 2.0, 12.0, ((0, 4), (1, 8)), jnp.float32)
    moment_second = jnp.clip(jnp.exp(math.log(100.0) - 4.6051702 * jax.random.uniform(arg_keys[9], (D, EXPERTS, H), jnp.float32) ** shard_levels(arg_keys[9], (D, EXPERTS, H), ((0, 4), (1, 8)), -0.2, 0.2)), 1.0, 100.0)
    return {"tokens": tokens, "cotangent": cotangent, "expert_ids": expert_ids, "combine": combine, "placement": placement, "swap_slots": swap_slots, "gate_weight": gate_weight, "up_weight": up_weight, "moment_first": moment_first, "moment_second": moment_second}


beta_first = 0.9
beta_second = 0.999
adam_steps = 10.0
epsilon = 1e-08

def migration_sources(swap_slots, holders, per_holder):
    slot_ids = jnp.arange(holders, dtype=jnp.int32)
    partner = jnp.bitwise_xor(slot_ids, holders // 2)
    local_ids = jnp.arange(per_holder, dtype=jnp.int32)[None, :]
    chosen = swap_slots[:, None] == local_ids
    from_holder = jnp.where(chosen, partner[:, None], slot_ids[:, None])
    from_slot = jnp.where(chosen, swap_slots[partner][:, None], local_ids)
    return (from_holder * per_holder + from_slot).reshape(-1).astype(jnp.int32)

def reference(tokens, cotangent, expert_ids, combine, placement, swap_slots, gate_weight, up_weight, moment_first, moment_second):
    sources = migration_sources(swap_slots, HOLDERS, EXP_DEV)
    moved = placement[sources]
    gate_moved = gate_weight[sources]
    up_moved = up_weight[sources]
    first_old = moment_first[:, sources]
    second_old = moment_second[:, sources]
    row_tokens = HOLDERS * TOK_DEV
    most_rows = HOLDERS * CAP

    def add_row(summed, row_index):
        offset_tok = (row_index * row_tokens).astype(jnp.int32)
        row_x = lax.dynamic_slice_in_dim(tokens, offset_tok, row_tokens, 0)
        row_dy = lax.dynamic_slice_in_dim(cotangent, offset_tok, row_tokens, 0)
        row_ids = lax.dynamic_slice_in_dim(expert_ids, offset_tok, row_tokens, 0).reshape(-1)
        row_weights = lax.dynamic_slice_in_dim(combine, offset_tok, row_tokens, 0).reshape(-1)
        sorted_ids = jnp.argsort(row_ids, stable=True).astype(jnp.int32)
        sorted_ids = jnp.concatenate([sorted_ids, jnp.zeros((most_rows,), jnp.int32)])
        counts = lax.optimization_barrier(jnp.sum((row_ids[:, None] == jnp.arange(EXPERTS, dtype=jnp.int32)[None, :]).astype(jnp.int32), axis=0))
        starts = (jnp.cumsum(counts) - counts).astype(jnp.int32)

        def slot_partial(slot):
            expert = moved[slot]
            picked = lax.dynamic_slice_in_dim(sorted_ids, starts[expert], most_rows, 0)
            live_rows = jnp.arange(most_rows, dtype=jnp.int32) < counts[expert]
            token_rows = picked // TOPK
            inputs = row_x[token_rows]
            scaled = jnp.where(live_rows, row_weights[picked], jnp.zeros((), row_weights.dtype))
            grads = (row_dy[token_rows].astype(jnp.float32) * scaled[:, None]).astype(jnp.bfloat16)
            gate_out = jnp.dot(inputs, gate_moved[slot].T, preferred_element_type=jnp.float32)
            up_out = jnp.dot(inputs, up_moved[slot].T, preferred_element_type=jnp.float32)
            hidden_act = (jax.nn.silu(gate_out) * up_out).astype(jnp.bfloat16)
            partial_sum = jnp.dot(grads.T, hidden_act, preferred_element_type=jnp.float32)
            rounded = lax.optimization_barrier(partial_sum.astype(jnp.bfloat16))
            return rounded.astype(jnp.float32)
        blocks = lax.map(slot_partial, jnp.arange(EXPERTS, dtype=jnp.int32))
        return (summed + blocks, None)
    zero_sums = jnp.zeros((EXPERTS, D, H), jnp.float32)
    summed, unused = lax.scan(add_row, zero_sums, jnp.arange(N_DP, dtype=jnp.int32))
    gradient = jnp.transpose(summed, (1, 0, 2))
    first_new = beta_first * first_old + (1.0 - beta_first) * gradient
    second_new = beta_second * second_old + (1.0 - beta_second) * gradient * gradient
    update = first_new / (1.0 - beta_first ** adam_steps) / (jnp.sqrt(second_new / (1.0 - beta_second ** adam_steps)) + epsilon)
    return (gate_moved, up_moved, first_new, second_new, update)
```

```python
import functools

import jax
import jax.numpy as jnp
from jax import lax
from jax.experimental import pallas as pl
from jax.experimental.pallas import tpu as pltpu
from jax.sharding import PartitionSpec as P

beta_first = 0.9
beta_second = 0.999
adam_steps = 10.0
epsilon = 1e-08
f32 = jnp.float32
bf16 = jnp.bfloat16
traded_chunks = 2


def exchange(block, axis, bit):
    count = lax.axis_size(axis)
    return lax.ppermute(block, axis, [(i, i ^ (1 << bit)) for i in range(count)])


def cuts(size, parts, step=16):
    edges = [size * c // parts // step * step for c in range(parts)] + [size]
    return list(zip(edges[:-1], edges[1:]))


def bits_of(count):
    return count.bit_length() - 1


def gather_rows(own, axis):
    have = [own]
    for bit in reversed(range(1, bits_of(lax.axis_size(axis)))):
        near = exchange(own, axis, bit)
        if len(have) > 1:
            rest = have[1] if len(have) == 2 else jnp.concatenate(have[1:], axis=0)
            have = have + [near, exchange(rest, axis, bit)]
        else:
            have = have + [near]
    mine = jnp.concatenate(have, axis=0)
    return mine, exchange(mine, axis, 0)


def gather_pieces(own, axis):
    count = lax.axis_size(axis)
    colours = bits_of(count)
    near = [exchange(own, axis, bit) for bit in range(colours)]
    parts = {}
    for colour, (low, high) in enumerate(cuts(own.shape[0], colours)):
        have = {0: own[low:high]}
        for step in range(colours):
            bit = (colour + step) % colours
            for key in list(have):
                if key == 0:
                    have[1 << bit] = near[bit][low:high]
                else:
                    have[key | 1 << bit] = exchange(have[key], axis, bit)
        for key, value in have.items():
            parts.setdefault(key, []).append(value)
    pieces = []
    for key in range(count):
        if key == 0:
            pieces.append(own)
        elif key & (key - 1) == 0:
            pieces.append(near[bits_of(key)])
        else:
            pieces.append(jnp.concatenate(parts[key], axis=0))
    return pieces


def scatter_sum(blocks, axis):
    count, rows = blocks.shape[0], blocks.shape[1]
    colours = bits_of(count)
    out = []
    for colour, (low, high) in enumerate(cuts(rows, colours)):
        current = {key: blocks[key, low:high] for key in range(count)}
        for step in range(colours):
            bit = (colour + step) % colours
            leave = [key for key in sorted(current) if key & (1 << bit)]
            sent = jnp.stack([current[key] for key in leave]).astype(bf16)
            got = exchange(sent, axis, bit).astype(f32)
            for at, key in enumerate(leave):
                kept = key ^ (1 << bit)
                current[kept] = current[kept] + got[at]
                del current[key]
        out.append(current[0])
    return jnp.concatenate(out, axis=0)


def relative(array, axis, width):
    me = lax.axis_index(axis)
    return jnp.concatenate(
        [
            lax.dynamic_slice_in_dim(array, (me ^ key) * width, width, 1)
            for key in range(lax.axis_size(axis))
        ],
        axis=1,
    )


def pack_kernel(slot_ref, first_ref, second_ref, first_out, second_out):
    slot = slot_ref[0]
    first_out[...] = first_ref[:, slot, :].astype(bf16)
    second_out[...] = second_ref[:, slot, :].astype(bf16)


def pack_moments(slot, first, second):
    rows, per_holder, width = first.shape
    tile = 128 if rows % 128 == 0 else rows
    whole = pl.BlockSpec((tile, per_holder, width), lambda i, s: (i, 0, 0))
    flat = pl.BlockSpec((tile, width), lambda i, s: (i, 0))
    return pl.pallas_call(
        pack_kernel,
        grid_spec=pltpu.PrefetchScalarGridSpec(
            num_scalar_prefetch=1,
            grid=(rows // tile,),
            in_specs=[whole, whole],
            out_specs=[flat, flat],
        ),
        out_shape=[jax.ShapeDtypeStruct((rows, width), bf16)] * 2,
        name="pack_moments",
    )(slot.reshape(1), first, second)


def adam_kernel(
    per_holder, slot_ref, first_ref, second_ref, first_in, second_in, *rest
):
    grads, (first_out, second_out, update_out) = rest[:per_holder], rest[per_holder:]
    traded = slot_ref[0]
    for s in range(per_holder):
        is_traded = traded == s
        old_first = jnp.where(is_traded, first_in[...].astype(f32), first_ref[:, s, :])
        old_second = jnp.where(is_traded, second_in[...].astype(f32), second_ref[:, s, :])
        gradient = grads[0][...]
        for other in range(1, per_holder):
            gradient = jnp.where(
                lax.rem(traded + other, per_holder) == s, grads[other][...], gradient
            )
        first_new = beta_first * old_first + (1.0 - beta_first) * gradient
        second_new = beta_second * old_second + (1.0 - beta_second) * gradient * gradient
        update = (
            first_new
            / (1.0 - beta_first**adam_steps)
            / (jnp.sqrt(second_new / (1.0 - beta_second**adam_steps)) + epsilon)
        )
        first_out[:, s, :] = first_new
        second_out[:, s, :] = second_new
        update_out[:, s, :] = update


def adam(slot, first, second, first_in, second_in, grads):
    rows, per_holder, width = first.shape
    tile = 64 if rows % 64 == 0 else rows
    whole = pl.BlockSpec((tile, per_holder, width), lambda i, s: (i, 0, 0))
    flat = pl.BlockSpec((tile, width), lambda i, s: (i, 0))
    return pl.pallas_call(
        functools.partial(adam_kernel, per_holder),
        grid_spec=pltpu.PrefetchScalarGridSpec(
            num_scalar_prefetch=1,
            grid=(rows // tile,),
            in_specs=[whole, whole, flat, flat] + [flat] * per_holder,
            out_specs=[whole] * 3,
        ),
        out_shape=[jax.ShapeDtypeStruct(first.shape, f32)] * 3,
        name="adam",
    )(slot.reshape(1), first, second, first_in, second_in, *grads)


def migration_sources(swap_slots, holders, per_holder):
    slot_ids = jnp.arange(holders, dtype=jnp.int32)
    partner = jnp.bitwise_xor(slot_ids, holders // 2)
    local_ids = jnp.arange(per_holder, dtype=jnp.int32)[None, :]
    chosen = swap_slots[:, None] == local_ids
    from_holder = jnp.where(chosen, partner[:, None], slot_ids[:, None])
    from_slot = jnp.where(chosen, swap_slots[partner][:, None], local_ids)
    return (from_holder * per_holder + from_slot).reshape(-1)


def swapped(block, axis, stride):
    count = lax.axis_size(axis)
    route = []
    for low in range(count):
        high = low | 1 << stride
        if high != low and high < count:
            route += [(low, high), (high, low)]
    return lax.ppermute(block, axis, route)


def per_device_routed(
    tokens,
    cotangent,
    expert_ids,
    combine,
    placement,
    swap_slots,
    gate_weight,
    up_weight,
    moment_first,
    moment_second,
):
    holders = lax.axis_size("expert")
    per_holder = gate_weight.shape[0]
    model_width = tokens.shape[1]
    experts = placement.shape[0]
    tok_dev = tokens.shape[0]
    top_count = expert_ids.shape[1]
    capacity = max(2, tok_dev * top_count * 5 // (4 * experts))
    own_index = lax.axis_index("expert")
    own_slot = swap_slots[own_index]
    outgoing = (
        lax.dynamic_index_in_dim(gate_weight, own_slot, 0, keepdims=False),
        lax.dynamic_index_in_dim(up_weight, own_slot, 0, keepdims=False),
        lax.dynamic_index_in_dim(moment_first, own_slot, 1, keepdims=False),
        lax.dynamic_index_in_dim(moment_second, own_slot, 1, keepdims=False),
    )
    incoming = (
        swapped(outgoing[0], "expert", holders.bit_length() - 2),
        swapped(outgoing[1], "expert", holders.bit_length() - 2),
        swapped(outgoing[2].astype(jnp.bfloat16), "expert", holders.bit_length() - 2).astype(
            jnp.float32
        ),
        swapped(outgoing[3].astype(jnp.bfloat16), "expert", holders.bit_length() - 2).astype(
            jnp.float32
        ),
    )
    gate_moved = lax.dynamic_update_index_in_dim(gate_weight, incoming[0], own_slot, 0)
    up_moved = lax.dynamic_update_index_in_dim(up_weight, incoming[1], own_slot, 0)
    first_old = lax.dynamic_update_index_in_dim(moment_first, incoming[2], own_slot, 1)
    second_old = lax.dynamic_update_index_in_dim(moment_second, incoming[3], own_slot, 1)
    sources = migration_sources(swap_slots, holders, per_holder)
    moved = placement[sources]
    slot_range = jnp.arange(experts, dtype=jnp.int32)
    matches = moved[:, None] == slot_range[None, :]
    slot_of = jnp.sum(jnp.where(matches, slot_range[:, None], 0), axis=0)
    flat_ids = expert_ids.reshape(-1)
    pair_count = flat_ids.shape[0]
    onehot = (flat_ids[:, None] == slot_range[None, :]).astype(jnp.int32)
    rank_ids = jnp.sum(jnp.cumsum(onehot, axis=0) * onehot, axis=1) - 1
    target = slot_of[flat_ids] * capacity + rank_ids
    source = (
        jnp.zeros((experts * capacity,), jnp.int32)
        .at[target]
        .set(jnp.arange(pair_count, dtype=jnp.int32) + 1)
    )
    filled = source > 0
    picked = jnp.maximum(source - 1, 0)
    token_rows = picked // top_count
    sent_tokens = jnp.where(filled[:, None], tokens[token_rows], jnp.zeros((), tokens.dtype))
    scaled = jnp.where(filled, combine.reshape(-1)[picked], 0.0)
    sent_grads = (cotangent[token_rows].astype(jnp.float32) * scaled[:, None]).astype(jnp.bfloat16)
    buffer_shape = (holders, per_holder, capacity, model_width)
    arrived_tokens, arrived_grads = (
        lax.all_to_all(
            sent_tokens.reshape(buffer_shape), "expert", split_axis=0, concat_axis=0, tiled=True
        ),
        lax.all_to_all(
            sent_grads.reshape(buffer_shape), "expert", split_axis=0, concat_axis=0, tiled=True
        ),
    )
    gate_part = jnp.einsum(
        "seck,ehk->sech",
        arrived_tokens,
        lax.all_gather(gate_moved, "dp", axis=2, tiled=True),
        preferred_element_type=jnp.float32,
    )
    up_part = jnp.einsum(
        "seck,ehk->sech",
        arrived_tokens,
        lax.all_gather(up_moved, "dp", axis=2, tiled=True),
        preferred_element_type=jnp.float32,
    )
    hidden_act = (jax.nn.silu(gate_part) * up_part).astype(jnp.bfloat16)
    gradient = lax.psum_scatter(
        jnp.einsum(
            "secd,sech->deh", arrived_grads, hidden_act, preferred_element_type=jnp.float32
        ).astype(jnp.bfloat16),
        "dp",
        scatter_dimension=0,
        tiled=True,
    ).astype(jnp.float32)
    first_new = beta_first * first_old + (1.0 - beta_first) * gradient
    second_new = beta_second * second_old + (1.0 - beta_second) * gradient * gradient
    update = (
        first_new
        / (1.0 - beta_first**adam_steps)
        / (jnp.sqrt(second_new / (1.0 - beta_second**adam_steps)) + epsilon)
    )
    return (gate_moved, up_moved, first_new, second_new, update)


def per_device_gathered(
    tokens,
    cotangent,
    expert_ids,
    combine,
    placement,
    swap_slots,
    gate_weight,
    up_weight,
    moment_first,
    moment_second,
):
    holders = lax.axis_size("expert")
    per_holder, hidden, width = gate_weight.shape
    model_width = tokens.shape[1]
    experts = placement.shape[0]
    far = bits_of(holders) - 1
    own_index = lax.axis_index("expert")
    own_slot = swap_slots[own_index]

    def slot_at(array, offset, dim=0):
        return lax.dynamic_index_in_dim(
            array, lax.rem(own_slot + offset, per_holder), dim, keepdims=False
        )

    moved = placement[migration_sources(swap_slots, holders, per_holder)]
    weight = jnp.zeros((tokens.shape[0], experts), f32)
    for j in range(expert_ids.shape[1]):
        weight = weight + jnp.where(
            expert_ids[:, j : j + 1] == moved[None, :], combine[:, j : j + 1], 0.0
        )
    high = lax.reduce_precision(weight, 8, 7)
    middle = lax.reduce_precision(weight - high, 8, 7)
    low = weight - high - middle
    terms = jnp.concatenate([high, middle, low], axis=1).astype(bf16)
    terms = jnp.pad(terms, ((0, 0), (0, -terms.shape[1] % 128)))
    sent_grads = jnp.concatenate([cotangent, terms], axis=1)

    row_tokens = jnp.concatenate(gather_rows(tokens, "expert"), axis=0)
    row_grads = jnp.concatenate(gather_rows(sent_grads, "expert"), axis=0)

    def pair(offset):
        return [slot_at(gate_weight, offset), slot_at(up_weight, offset)]

    stays = [
        gather_pieces(jnp.concatenate(pair(offset), axis=0), "dp")
        for offset in range(1, per_holder)
    ]
    gate_out, up_out = pair(0)
    gate_in, up_in, trades = [], [], []
    for begin, end in cuts(hidden, traded_chunks):
        block = jnp.concatenate([gate_out[begin:end], up_out[begin:end]], axis=0)
        block = exchange(block, "expert", far)
        gate_in.append(block[: end - begin])
        up_in.append(block[end - begin :])
        trades.append(gather_pieces(block, "dp"))
    gate_moved = lax.dynamic_update_index_in_dim(
        gate_weight, jnp.concatenate(gate_in, axis=0), own_slot, 0
    )
    up_moved = lax.dynamic_update_index_in_dim(
        up_weight, jnp.concatenate(up_in, axis=0), own_slot, 0
    )
    first_sent, second_sent = pack_moments(own_slot, moment_first, moment_second)
    first_in = exchange(first_sent, "expert", far)
    second_in = exchange(second_sent, "expert", far)

    x = relative(row_tokens, "dp", width)
    dy = relative(row_grads, "dp", width)
    terms = row_grads[:, model_width:].astype(f32)
    terms = terms[:, :experts] + terms[:, experts : 2 * experts] + terms[:, 2 * experts : 3 * experts]

    def gradient_of(pieces, offset):
        slot = own_index * per_holder + lax.rem(own_slot + offset, per_holder)
        scale = lax.dynamic_slice_in_dim(terms, slot, 1, 1)
        both = lax.dot_general(
            x,
            jnp.concatenate(pieces, axis=1),
            (((1,), (1,)), ((), ())),
            preferred_element_type=f32,
        )
        half = both.shape[1] // 2
        act = (jax.nn.silu(both[:, :half]) * both[:, half:] * scale).astype(bf16)
        partial = lax.dot_general(dy, act, (((0,), (0,)), ((), ())), preferred_element_type=f32)
        return scatter_sum(partial.reshape(-1, width, half), "dp")

    grads = [gradient_of(pieces, at + 1) for at, pieces in enumerate(stays)]
    grads = [
        jnp.concatenate([gradient_of(pieces, 0) for pieces in trades], axis=1)
    ] + grads
    first_new, second_new, update = adam(
        own_slot, moment_first, moment_second, first_in, second_in, grads
    )
    return (gate_moved, up_moved, first_new, second_new, update)


def solution(mesh):
    holders = mesh.shape["expert"]
    per_device = per_device_gathered if holders <= 8 else per_device_routed
    tokens = P(("dp", "expert"), None)
    weights = P("expert", None, "dp")
    moments = P("dp", "expert", None)
    return jax.shard_map(
        per_device,
        mesh=mesh,
        in_specs=(tokens,) * 4 + (P(), P()) + (weights,) * 2 + (moments,) * 2,
        out_specs=(weights,) * 2 + (moments,) * 3,
        check_vma=False,
    )
```
